256 devices in a mesh: row: 32 (over y, z_lo, core), col: 8 (over z_hi, x).
Axes of the slice: x: 4, y: 4, z: 8 (z_hi: 2, z_lo: 4; z = z_hi * 4 + z_lo), core: 2. Of those that a mesh axis runs over, the one named last changes fastest.
Arguments:
- integrals: bfloat16 [32768, 32768], P('row', 'col'), may hold values from -0.03125 to 0.03125
- amplitudes: bfloat16 [32768, 1024], P(('col', 'row')), may hold values from -6 to 6
- source: float32 [32768, 1024], P(('row', 'col')), may hold values from -6 to 6
- occ_energy: float32 [64], replicated, may hold values from -2.5 to -0.5
- vir_energy: float32 [512], replicated, may hold values from 0.3 to 3
- col_energy: float32 [1024], replicated, may hold values from 0.8 to 3
Outputs:
- new_amplitudes: float32 [32768, 1024], P(('row', 'col'))
The draws below stay inside these ranges and needn't reach their ends.
All inputs are finite; a program needn't handle non-finite values.
Results may differ from the reference program's by a relative error of at most 0.0003.
Values may be sent and summed in bfloat16 or wider, within the bound.
No kernel may reach another device: no remote copies, remote signals or barrier semaphores. Data moves between devices by JAX's collectives and lax.ppermute only.
A program may use at most 128 MiB of HBM per device.

```python
import math
import jax
import jax.numpy as jnp
from jax import lax

OCC = 64
VIRT = 512
COLS = 1024
PAIRS = 32768


def levels(stream_key, extent, split, low, largest):
    factor_of, own = 1.0, jax.random.fold_in(stream_key, 6)
    for axis_at, shards_of in split:
        steps = jnp.exp(jax.random.uniform(jax.random.fold_in(own, axis_at), (shards_of,), jnp.float32, low / len(split), largest / len(split)))
        factor_of = factor_of * jnp.repeat(steps, extent[axis_at] // shards_of).reshape([-1 if axis == axis_at else 1 for axis in range(len(extent))])
    return factor_of


def bell_draw(stream_key, shape, deviation, most, pieces=(), held_as=jnp.bfloat16):
    values = jax.random.normal(stream_key, shape, jnp.float32) * deviation
    if len(pieces) > 0:
        values = levels(stream_key, shape, pieces, -0.22, 0.18) * values
    return jnp.clip(values, min=-most, max=most).astype(held_as)


def setup_inputs(seed: int = 0) -> dict:
    splits = jax.random.split(jax.random.key(seed), 7)
    integrals = bell_draw(splits[0], (PAIRS, PAIRS), PAIRS ** -0.5, 0.03125, ((0, 32), (1, 8)))
    amplitudes = bell_draw(splits[1], (PAIRS, COLS), 1.0, 6.0, ((0, 256),))
    source = bell_draw(splits[2], (PAIRS, COLS), 1.0, 6.0, ((0, 256),), jnp.float32)
    occ_energy = jnp.clip(jax.random.uniform(splits[3], (OCC,), jnp.float32, -2.5, -0.5), -2.5, -0.5)
    vir_energy = jnp.clip(jnp.exp(jax.random.uniform(splits[4], (VIRT,), jnp.float32, math.log(0.3), math.log(3.0))), 0.3, 3.0)
    col_energy = jnp.clip(jax.random.uniform(splits[5], (COLS,), jnp.float32, 0.8, 3.0), 0.8, 3.0)
    return {"integrals": integrals, "amplitudes": amplitudes, "source": source, "occ_energy": occ_energy, "vir_energy": vir_energy, "col_energy": col_energy}


def reference(integrals, amplitudes, source, occ_energy, vir_energy, col_energy):
    cycle_term = jnp.dot(integrals, amplitudes, preferred_element_type=jnp.float32)
    blocks = integrals.reshape(OCC, VIRT, OCC, VIRT)
    amp_blocks = amplitudes.astype(jnp.float32).reshape(OCC, VIRT, COLS)

    def one_occupied(block):
        return jnp.einsum("bja,jbc->ac", block.astype(jnp.float32), amp_blocks, precision=lax.Precision.HIGHEST)

    exchange_term = lax.map(one_occupied, blocks).reshape(PAIRS, COLS)
    denom = vir_energy[None, :, None] - occ_energy[:, None, None] + col_energy[None, None, :]
    denom = denom.reshape(PAIRS, COLS)
    return -(source + cycle_term + exchange_term) / denom
```

```python
import jax
import jax.numpy as jnp
import numpy as np
from jax import lax
from jax.experimental import pallas as pl
from jax.experimental.pallas import tpu as pltpu
from jax.sharding import PartitionSpec as P

VIRT = 512
ROWS, COLS = 32, 8
F8 = jnp.float8_e4m3fn
CHUNKS = (256, 256, 256, 256)
GATHER = ((2 << 1, 1 << 1), (1 << 1, 2 << 1), (1 << 3, 3 << 3), (3 << 3, 1 << 3))
REDUCE = ((1, 3), (3, 1))
SCALE = 8.0
LO = 2.0**17
A8 = 64.0


def row_perm(step):
    return [(r, r ^ step[r & 1]) for r in range(ROWS)]


def all_perm(step):
    pairs = []
    for r in range(ROWS):
        for c in range(COLS):
            pairs.append((r * COLS + c, r * COLS + (c ^ step[r & 1])))
    return pairs


def piece_table():
    table = np.zeros((ROWS, ROWS), np.int32)
    for r in range(ROWS):
        for p in range(ROWS):
            at = r ^ (p >> 4)
            for bit, step in enumerate(GATHER):
                if (p >> bit) & 1:
                    at ^= step[at & 1]
            table[r, p] = at
    return table


def tile_table():
    table = np.zeros((2, COLS, 8), np.int32)
    for core in range(2):
        for c in range(COLS):
            for q in range(8):
                q0, q1, q2 = q >> 2, (q >> 1) & 1, q & 1
                at = c ^ (q2 << 2)
                if q0:
                    at ^= REDUCE[0][core]
                if q1:
                    at ^= REDUCE[1][core]
                table[core, c, q] = at
    return table


def prep_kernel(x_ref, hi_ref, lo_ref):
    x = x_ref[...]
    both = (x.astype(jnp.float32) + x.T.astype(jnp.float32)) * SCALE
    hi = both.astype(jnp.bfloat16)
    hi_ref[...] = hi
    lo_ref[...] = ((both - hi.astype(jnp.float32)) * LO).astype(F8)


def prep(integrals):
    rows, depth = integrals.shape
    spec = pl.BlockSpec((VIRT, VIRT), lambda i, j: (i, j))
    return pl.pallas_call(
        prep_kernel,
        grid=(rows // VIRT, depth // VIRT),
        in_specs=[spec],
        out_specs=[spec, spec],
        out_shape=[
            jax.ShapeDtypeStruct((rows, depth), jnp.bfloat16),
            jax.ShapeDtypeStruct((rows, depth), F8),
        ],
        cost_estimate=pl.CostEstimate(flops=0, bytes_accessed=rows * depth * 5, transcendentals=0),
        name="prep",
    )(integrals)


def mm_kernel(table, hi_ref, lo_ref, mine, other, o_ref, a, a8, sems):
    block = mine.shape[0] // 16

    @pl.when(pl.program_id(0) == 0)
    def _():
        copies = []
        for p in range(32):
            src = mine if p < 16 else other
            at = pl.multiple_of(table[8 + p] * block, block)
            copies.append(
                pltpu.make_async_copy(
                    src.at[pl.ds((p % 16) * block, block)], a.at[pl.ds(at, block)], sems.at[p]
                )
            )
        for copy in copies:
            copy.start()
        for copy in copies:
            copy.wait()
        a8[...] = (a[...].astype(jnp.float32) * A8).astype(F8)

    main = jnp.dot(hi_ref[...], a[...], preferred_element_type=jnp.float32)
    rest = jnp.dot(lo_ref[...], a8[...], preferred_element_type=jnp.float32)
    o_ref[...] = main + rest * (1.0 / (LO * A8))


def mm(hi, lo, mine, other, table, half):
    depth, cols = hi.shape[1], mine.shape[1]
    tile = hi.shape[0] // 8
    m_spec = pl.BlockSpec((tile, depth), lambda i, t: (t[i + 4 * half], 0))
    hbm = pl.BlockSpec(memory_space=pl.ANY)
    return pl.pallas_call(
        mm_kernel,
        grid_spec=pltpu.PrefetchScalarGridSpec(
            num_scalar_prefetch=1,
            grid=(4,),
            in_specs=[m_spec, m_spec, hbm, hbm],
            out_specs=pl.BlockSpec((tile, cols), lambda i, t: (i, 0)),
            scratch_shapes=[
                pltpu.VMEM((depth, cols), jnp.bfloat16),
                pltpu.VMEM((depth, cols), F8),
                pltpu.SemaphoreType.DMA((32,)),
            ],
        ),
        out_shape=jax.ShapeDtypeStruct((4 * tile, cols), jnp.float32),
        cost_estimate=pl.CostEstimate(
            flops=12 * tile * depth * cols, bytes_accessed=tile * depth * 12, transcendentals=0
        ),
        name="mm",
    )(table, hi, lo, mine, other)


def gather(block):
    for step in GATHER:
        block = jnp.concatenate([block, lax.ppermute(block, "row", row_perm(step))], axis=0)
    return block, lax.ppermute(block, "row", row_perm((1, 1)))


def swap(value, step):
    sent = value.astype(jnp.float16)
    return lax.ppermute(sent, ("row", "col"), all_perm(step)).astype(jnp.float32)


def per_device(integrals, amplitudes, source, occ_energy, vir_energy, col_energy):
    row, col = lax.axis_index("row"), lax.axis_index("col")
    tiles = jnp.asarray(tile_table())[row & 1, col]
    pieces = jnp.asarray(piece_table())[row]
    table = jnp.concatenate([tiles, pieces])
    out_rows = source.shape[0]
    hi, lo = prep(integrals)
    sums = []
    start = 0
    for width in CHUNKS:
        mine, other = gather(amplitudes[:, start : start + width])
        send = mm(hi, lo, mine, other, table, 1)
        got = swap(send, REDUCE[0])
        keep = mm(hi, lo, mine, other, table, 0)
        half = 2 * out_rows
        got = swap(keep[half:] + got[half:], REDUCE[1]) + (keep[:half] + got[:half])
        sums.append(swap(got[out_rows:], (4, 4)) + got[:out_rows])
        start += width
    summed = jnp.concatenate(sums, axis=1) * (1.0 / SCALE)
    first = (row * COLS + col) * out_rows
    vir_all = jnp.tile(vir_energy, occ_energy.shape[0])
    occ_all = jnp.repeat(occ_energy, VIRT)
    vir_part = lax.dynamic_slice_in_dim(vir_all, first, out_rows, 0)
    occ_part = lax.dynamic_slice_in_dim(occ_all, first, out_rows, 0)
    denom = vir_part[:, None] - occ_part[:, None] + col_energy[None, :]
    return -(source + summed) / denom


def solution(mesh):
    in_specs = (P("row", "col"), P(("col", "row"), None), P(("row", "col"), None), P(), P(), P())
    out_specs = P(("row", "col"), None)
    return jax.shard_map(
        per_device, mesh=mesh, in_specs=in_specs, out_specs=out_specs, check_vma=False
    )
```

```python
import functools

import jax
import jax.numpy as jnp
from jax import lax
from jax.experimental import pallas as pl
from jax.experimental.pallas import tpu as pltpu
from jax.sharding import PartitionSpec as P

VIRT = 512
ROWS, COLS = 32, 8
F8 = jnp.float8_e4m3fn
CHUNKS = (256, 384, 384)
FAR = ((0,), (1,), (2,))
GATHER = ((2 << 1, 1 << 1), (1 << 1, 2 << 1), (1 << 3, 3 << 3), (3 << 3, 1 << 3))
REDUCE = ((1, 3), (3, 1))
SCALE = 8.0
LO = 2.0**17
A8 = 64.0
PREP_LIMIT = 56
MM_LIMIT = 32


def row_perm(step):
    return [(r, r ^ step[r & 1]) for r in range(ROWS)]


def all_perm(step):
    pairs = []
    for r in range(ROWS):
        for c in range(COLS):
            pairs.append((r * COLS + c, r * COLS + (c ^ step[r & 1])))
    return pairs


def bits(value):
    return value & 1, (value >> 1) & 1


def piece_at(piece, row):
    core = piece & 1
    z0, z1 = bits((piece ^ row) >> 1)
    y0, y1 = bits((piece ^ row) >> 3)
    first, second = z1 + 2 * z0, z0 + 2 * z1
    turn, walk = (y0 ^ y1) * 4 + y1 * 8, y1 * 4 + (y0 ^ y1) * 8
    place = jnp.where(core == 0, first + turn, second + walk)
    return place + ((piece ^ row) & 1) * 16


def tile_at(dest, row, col):
    x0, x1 = bits((dest ^ col) & 3)
    even = (x0 ^ x1) * 2 + x1
    odd = x1 * 2 + (x0 ^ x1)
    return jnp.where((row & 1) == 0, even, odd)


VMEM = pl.BlockSpec(memory_space=pltpu.VMEM)
ANY = pl.BlockSpec(memory_space=pl.ANY)


def prep_kernel(occ, x_hbm, *refs):
    hi_hbm, lo_hbm, x_ref, hi_ref, lo_ref, in_sems, out_sems = refs[2 * occ :]
    row, col = lax.axis_index("row"), lax.axis_index("col")
    depth = x_hbm.shape[1]
    side = VIRT // 4
    count = depth // VIRT
    loads = []
    for j in range(count):
        span = pl.ds(j * VIRT, VIRT)
        part = x_hbm.at[pl.ds(occ * VIRT, VIRT), span]
        loads.append(pltpu.make_async_copy(part, x_ref.at[:, span], in_sems.at[j]))
        loads[-1].start()
    stores = []
    for g in range(count):
        loads[g].wait()
        x = x_ref[:, g * VIRT : (g + 1) * VIRT]
        both = (x.astype(jnp.float32) + x.T.astype(jnp.float32)) * SCALE
        hi = both.astype(jnp.bfloat16)
        lo = ((both - hi.astype(jnp.float32)) * LO).astype(F8)
        for u in range(4):
            over = pl.ds(pl.multiple_of(piece_at(g * 4 + u, row) * side, side), side)
            for s in range(4):
                down = pl.ds(pl.multiple_of(tile_at(s, row, col) * side, side), side)
                part = (slice(s * side, (s + 1) * side), slice(u * side, (u + 1) * side))
                hi_ref[down, over] = hi[part]
                lo_ref[down, over] = lo[part]
            for n, (src, dst) in enumerate(((hi_ref, hi_hbm), (lo_ref, lo_hbm))):
                sem = out_sems.at[n, g * 4 + u]
                to = dst.at[occ, :, over]
                stores.append(pltpu.make_async_copy(src.at[:, over], to, sem))
                stores[-1].start()
    for store in stores:
        store.wait()


def prep(integrals, occ, old=()):
    depth = integrals.shape[1]
    hi = jax.ShapeDtypeStruct((10, VIRT, depth), jnp.bfloat16)
    lo = jax.ShapeDtypeStruct((18, VIRT, depth), F8)
    return pl.pallas_call(
        functools.partial(prep_kernel, occ),
        in_specs=[ANY] * (1 + len(old)),
        out_specs=[ANY, ANY],
        out_shape=[hi, lo],
        scratch_shapes=[
            pltpu.VMEM((VIRT, depth), jnp.bfloat16),
            pltpu.VMEM((VIRT, depth), hi.dtype),
            pltpu.VMEM((VIRT, depth), lo.dtype),
            pltpu.SemaphoreType.DMA((depth // VIRT,)),
            pltpu.SemaphoreType.DMA((2, ROWS)),
        ],
        input_output_aliases={1 + n: n for n in range(len(old))},
        compiler_params=pltpu.CompilerParams(vmem_limit_bytes=PREP_LIMIT << 20),
        cost_estimate=pl.CostEstimate(
            flops=0, bytes_accessed=VIRT * depth * 10, transcendentals=0
        ),
        name="prep",
    )(integrals, *old)


def base_kernel(vir, occ, out):
    place = lax.axis_index("row") * COLS + lax.axis_index("col")
    per_occ = vir.shape[0]
    out[...] = vir[pl.ds(place % per_occ, 1), :] - occ[place // per_occ]


def base(vir_energy, occ_energy, out_rows):
    return pl.pallas_call(
        base_kernel,
        in_specs=[VMEM, pl.BlockSpec(memory_space=pltpu.SMEM)],
        out_specs=VMEM,
        out_shape=jax.ShapeDtypeStruct((1, out_rows), jnp.float32),
        compiler_params=pltpu.CompilerParams(vmem_limit_bytes=1 << 20),
        name="base",
    )(vir_energy.reshape(-1, out_rows), occ_energy)


def mm_kernel(spans, hi_hbm, lo_hbm, *refs):
    count = len(spans)
    pieces, (send, keep, hi, lo, sems) = refs[:count], refs[count:]
    depth = pieces[0].shape[0]
    side = VIRT // 4
    last = count - 1

    def copies(i, k):
        span = pl.ds(spans[k], depth)
        return [
            pltpu.make_async_copy(src.at[i, :, span], dst.at[k], sems.at[k, m])
            for m, (src, dst) in enumerate(((hi_hbm, hi), (lo_hbm, lo)))
        ]

    def begin(i, k):
        for copy in copies(i, k):
            copy.start()

    for k in range(last):
        begin(0, k)
    values = [piece[...] for piece in pieces]
    small = [(value.astype(jnp.float32) * A8).astype(F8) for value in values]

    @pl.loop(0, 2)
    def _(i):
        total = None
        for k in range(count):
            for copy in copies(i, k):
                copy.wait()
            if k == 0:
                begin(i, last)
            else:
                pl.when(i == 0)(functools.partial(begin, 1, k - 1))
            part = jnp.dot(hi[k], values[k], preferred_element_type=jnp.float32)
            rest = jnp.dot(lo[k], small[k], preferred_element_type=jnp.float32)
            part = part + rest * (1.0 / (LO * A8))
            total = part if k == 0 else total + part
        for q in range(4):
            (keep, send)[q // 2][q % 2, i] = total[q * side : (q + 1) * side]


def mm(tops, spans, pieces):
    depth, cols = pieces[0].shape
    count = len(spans)
    out = jax.ShapeDtypeStruct((2, 2, VIRT // 4, cols), jnp.float32)
    return pl.pallas_call(
        functools.partial(mm_kernel, spans),
        in_specs=[ANY] * 2 + [VMEM] * count,
        out_specs=[VMEM] * 2,
        out_shape=[out] * 2,
        scratch_shapes=[
            pltpu.VMEM((count, VIRT, depth), jnp.bfloat16),
            pltpu.VMEM((count, VIRT, depth), F8),
            pltpu.SemaphoreType.DMA((count, 2)),
        ],
        compiler_params=pltpu.CompilerParams(vmem_limit_bytes=MM_LIMIT << 20),
        cost_estimate=pl.CostEstimate(
            flops=6 * VIRT * 2 * depth * cols * count,
            bytes_accessed=6 * count * VIRT * depth,
            transcendentals=0,
        ),
        name="mm",
    )(*tops, *pieces)


def gather(block):
    for n, step in enumerate(GATHER):
        got = lax.ppermute(block, "row", row_perm(step))
        if n < 3:
            block = jnp.concatenate([block, got], axis=0)
    other = lax.ppermute(block, "row", row_perm((1, 1)))
    late = lax.ppermute(got, "row", row_perm((1, 1)))
    return (block, other), (got, late)


def swap(value, step):
    sent = value.astype(jnp.float16)
    got = lax.ppermute(sent, ("row", "col"), all_perm(step))
    return got.astype(jnp.float32)


def body(integrals, amplitudes, source, occ_energy, vir_energy, col_energy):
    col = lax.axis_index("col")
    out_rows = source.shape[0]
    tops = ()
    for occ in range(2):
        tops = prep(integrals, occ, tuple(tops))
    below = base(vir_energy, occ_energy, out_rows)[0]
    halves = []
    start = 0
    for width in CHUNKS:
        early, late = gather(amplitudes[:, start : start + width])
        depth = early[0].shape[0]
        send, keep = mm(tops, (0, 2 * depth, depth, 3 * depth), early + late)
        keep = keep + swap(send, REDUCE[0])
        keep = keep[0] + swap(keep[1], REDUCE[1])
        near = lax.dynamic_index_in_dim(keep, col // 4, 0, keepdims=False)
        far = lax.dynamic_index_in_dim(keep, 1 - col // 4, 0, keepdims=False)
        halves.append((near, far))
        start += width
    done = []
    for group in FAR:
        near, far = (jnp.concatenate([halves[n][m] for n in group], axis=1) for m in range(2))
        done.append(near + swap(far, (4, 4)))
    summed = jnp.concatenate(done, axis=1) * (1.0 / SCALE)
    denom = below[:, None] + col_energy[None, :]
    return -(source + summed) / denom


def solution(mesh):
    in_specs = (P("row", "col"), P(("col", "row"), None), P(("row", "col"), None), P(), P(), P())
    out_specs = P(("row", "col"), None)
    return jax.shard_map(body, mesh=mesh, in_specs=in_specs, out_specs=out_specs, check_vma=False)
```
